256 devices in a mesh: sect: 2 (over core), gy: 16 (over x, y), gx: 8 (over z).
Axes of the slice: x: 4, y: 4, z: 8, core: 2. Of those that a mesh axis runs over, the one named last changes fastest.
Arguments:
- adjoint_init: float32 [2, 32, 512, 2048], P('sect', None, 'gy', 'gx'), may hold values from -6 to 6
- diffusivity: float32 [2, 512, 2048], P('sect', 'gy', 'gx'), may hold values from 0.02 to 0.12
- mixing: float32 [2, 32, 32], P('sect'), may hold values from -0.75 to 0.75
- coupling: float32 [2, 32, 8], P('sect'), may hold values from -6 to 6
- history: float32 [2, 4, 4, 512, 2048], P('sect', None, None, 'gy', 'gx'), may hold values from -6 to 6
- extract: float32 [4, 32], replicated, may hold values from -3 to 3
- land_mask: int32 [512, 2048], P('gy', 'gx'), may hold values 0 or 1
- regrid: float32 [128, 128, 128], P(('gy', 'gx')), may hold values from -0.5 to 0.5
- atmos_tile_index: int32 [16384, 1], replicated, may hold values from 0 to 127; in each aligned block of 128 rows (0 to 127, 128 to 255, ...) at most 2 rows name the same one
- ocean_block_index: int32 [16384], replicated, may hold values from 0 to 63
- atmos_block_index: int32 [16384], replicated, may hold values from 0 to 63
Outputs:
- adjoint_state: float32 [2, 32, 512, 2048], P('sect', None, 'gy', 'gx')
The draws below stay inside these ranges and needn't reach their ends.
Inputs may be any that keep to these rules, and one draw needn't show every extreme that they name: `atmos_tile_index`: list rows i*128 to (i+1)*128 - 1 are ocean tile i's entries; among them at most 2 name the same atmosphere tile, and exactly 2 do so for some atmosphere tile.
All inputs are finite; a program needn't handle non-finite values. No bound on the sum of `land_mask` on one device may be relied on, other than what follows from the above.
Results may differ from the reference program's by a relative error of at most 0.0001.
Values sent between devices are 32-bit elements; how exact they have to be, the bound alone decides.
A program may use at most 64 MiB of HBM per device.

```python
import math
import jax
import jax.numpy as jnp
import numpy as np
from jax import lax

COUPLING_FIELDS = 4
WINDOW_STEPS = 4
BLOCK_GRID_CELLS = 128
CY = 32
CX = 256
REGRID_ENTRIES = 128
NC = 32
SECTION_TILES = 128
CAP = 2
TILE_BLOCKS = 64
NY = 512
NX = 2048
N_GY = 16
N_GX = 8


def place_ends(entries, stream_key, low, high):
    longest = entries.shape.index(max(entries.shape))
    spots = []
    for shift in (0, 1):
        where = [jax.random.randint(jax.random.fold_in(stream_key, axis), (), 0, length) for axis, length in enumerate(entries.shape)]
        where[longest] = (where[longest] + shift) % entries.shape[longest]
        spots.append(tuple(where))
    return entries.at[spots[0]].set(low).at[spots[1]].set(high)


def levels(stream_key, extent, shards, smallest, top_value):
    def one(position, blocks):
        heights = jax.random.uniform(jax.random.fold_in(jax.random.fold_in(stream_key, 6), position), (blocks,), jnp.float32, smallest / len(shards), top_value / len(shards))
        return jnp.repeat(jnp.exp(heights), extent[position] // blocks).reshape((-1,) + (1,) * (len(extent) - position - 1))

    level = one(*shards[0])
    for cut in shards[1:]:
        level = level * one(*cut)
    return level


def deal_out(own_key, own, number, rows, count, top, bound, skew):
    order = jax.random.permutation(own_key, count)
    crowded, usual = portions_of(count, rows * top, bound, skew, True), portions_of(count, rows * top, bound, skew, False)
    places = jnp.arange(count)

    def named(tallies, rotation):
        used = int((tallies > 0).sum())
        fixed = max(1, used // 4)
        shifted = fixed + (places - fixed + rotation * (used - fixed)) % max(1, count - fixed)
        return jnp.zeros((count,), jnp.int32).at[order[jnp.where(places < fixed, places, shifted)]].set(jnp.asarray(tallies, jnp.int32))

    tallies = jnp.where(number % 4 == 0, named(crowded, number // 4), named(usual, number - number // 4 - 1))
    mixed = jax.random.permutation(jax.random.fold_in(own, 3), count)
    giver, taker = mixed[0:count // 2 * 2:2], mixed[1:count // 2 * 2:2]
    room = jnp.minimum(tallies[giver] - 1, bound - tallies[taker]) // 2
    room = jnp.where((giver == order[0]) | (taker == order[0]) | (tallies[taker] == 0), 0, jnp.maximum(room, 0))
    shifted = jax.random.randint(jax.random.fold_in(own, 4), (count // 2,), 0, 1 << 20) % (room + 1)
    tallies = tallies.at[giver].add(-shifted).at[taker].add(shifted)
    members = jnp.searchsorted(jnp.cumsum(tallies), jnp.arange(rows * top), side="right").astype(jnp.int32)
    grid = members.reshape(top, rows).T
    grid = grid[jax.random.permutation(jax.random.fold_in(own, 1), rows)]
    rotation = jax.random.randint(jax.random.fold_in(own, 2), (rows, 1), 0, top)
    return jnp.take_along_axis(grid, (jnp.arange(top)[None, :] + rotation) % top, axis=1)


def portions_of(number_of, total, bound, skew, full):
    loads = [(1 << 20) // math.isqrt(grade ** skew) + 1 for grade in range(1, number_of + 1)]
    largest = bound if full else min(bound, max(-(-total // number_of), total * loads[0] // sum(loads)))
    least = 1 if total - largest >= number_of - 1 else 0
    counts, surplus = [largest] + [least] * (number_of - 1), total - largest - least * (number_of - 1)
    while surplus > 0:
        movable = [i for i in range(1, number_of) if counts[i] < largest] or [i for i in range(1, number_of) if counts[i] < bound]
        pool, budget = sum([loads[i] for i in movable]), surplus
        for i in movable:
            more = min(bound - counts[i], max(1, budget * loads[i] // pool), surplus)
            counts[i] = counts[i] + more
            surplus = surplus - more
    return np.array(counts)


def noise(stream_key, dims, width, bound, split=(), kind=jnp.bfloat16):
    values = width * jax.random.normal(stream_key, dims, jnp.float32)
    if split:
        values = values * levels(stream_key, dims, split, -0.22, 0.18)
    return jnp.clip(values, -bound, bound).astype(kind)


def setup_inputs(seed: int = 0) -> dict:
    seeds = jax.random.split(jax.random.key(seed), 12)
    adjoint_init = noise(seeds[0], (2, NC, NY, NX), 1.0, 6.0, ((0, 2), (2, 16), (3, 8)), jnp.float32)
    diffusivity = jnp.clip(jnp.exp(math.log(0.12) - 1.7917595 * jax.random.uniform(seeds[1], (2, NY, NX), jnp.float32) ** levels(seeds[1], (2, NY, NX), ((0, 2), (1, 16), (2, 8)), -0.2, 0.2)), 0.02, 0.12)
    mixing = noise(seeds[2], (2, NC, NC), 0.05, 0.75, ((0, 2),), jnp.float32)
    coupling = noise(seeds[3], (2, NC, 2 * COUPLING_FIELDS), 0.5, 6.0, ((0, 2),), jnp.float32)
    history = noise(seeds[4], (2, WINDOW_STEPS, COUPLING_FIELDS, NY, NX), 1.0, 6.0, ((0, 2), (3, 16), (4, 8)), jnp.float32)
    extract = noise(seeds[5], (COUPLING_FIELDS, NC), 0.2, 3.0, (), jnp.float32)
    land_mask = place_ends((jax.random.randint(seeds[6], (NY, NX), 0, 4) < 3).astype(jnp.int32), jax.random.fold_in(seeds[6], 1), 0, 1)
    regrid = noise(seeds[7], (SECTION_TILES, BLOCK_GRID_CELLS, BLOCK_GRID_CELLS), BLOCK_GRID_CELLS ** -0.5, 0.5, ((0, 128),), jnp.float32)
    atmos_tile_index_keys = jax.random.split(jax.random.fold_in(seeds[8], 1), (SECTION_TILES * REGRID_ENTRIES) // REGRID_ENTRIES)
    atmos_tile_index_turns = jax.random.permutation(jax.random.fold_in(seeds[8], 3), (SECTION_TILES * REGRID_ENTRIES) // REGRID_ENTRIES)
    atmos_tile_index = jax.vmap(lambda own, number: deal_out(jax.random.fold_in(seeds[8], 2), own, number, REGRID_ENTRIES, SECTION_TILES, 1, CAP, 2))(atmos_tile_index_keys, atmos_tile_index_turns).reshape((SECTION_TILES * REGRID_ENTRIES, 1))
    ocean_block_index = place_ends(jax.random.randint(seeds[9], (SECTION_TILES * REGRID_ENTRIES,), 0, TILE_BLOCKS), jax.random.fold_in(seeds[9], 1), 0, TILE_BLOCKS - 1).astype(jnp.int32)
    atmos_block_index = place_ends(jax.random.randint(seeds[10], (SECTION_TILES * REGRID_ENTRIES,), 0, TILE_BLOCKS), jax.random.fold_in(seeds[10], 1), 0, TILE_BLOCKS - 1).astype(jnp.int32)
    return {"adjoint_init": adjoint_init, "diffusivity": diffusivity, "mixing": mixing, "coupling": coupling, "history": history, "extract": extract, "land_mask": land_mask, "regrid": regrid, "atmos_tile_index": atmos_tile_index, "ocean_block_index": ocean_block_index, "atmos_block_index": atmos_block_index}


def laplace(field):
    padded = jnp.pad(field, ((0, 0), (1, 1), (0, 0)))
    return (padded[:, 2:, :] + padded[:, :-2, :] + jnp.roll(field, 1, axis=2)
            + jnp.roll(field, -1, axis=2) - 4.0 * field)


def advance(adjoint, wet_mask, diffusive, mixing_m, coupling_m, forcing):
    masked = wet_mask * adjoint
    spread = laplace(diffusive * masked)
    mixing_term = jnp.einsum("dc,dyx->cyx", mixing_m, masked, precision=lax.Precision.HIGHEST)
    forced = jnp.einsum("cq,qyx->cyx", coupling_m, forcing, precision=lax.Precision.HIGHEST)
    return masked + spread + mixing_term + forced


def regrid_surface(surfaces, regrid, atmos_tile_index, ocean_block_index, atmos_block_index):
    per_tile_layout = surfaces.reshape(WINDOW_STEPS, COUPLING_FIELDS, N_GY, CY, N_GX, CX).transpose(2, 4, 0, 1, 3, 5)
    per_tile_layout = per_tile_layout.reshape(SECTION_TILES, WINDOW_STEPS, COUPLING_FIELDS, TILE_BLOCKS, BLOCK_GRID_CELLS)
    sources = ocean_block_index.reshape(SECTION_TILES, REGRID_ENTRIES).astype(jnp.int32)
    picked = jax.vmap(lambda tile_data, index_row: jnp.take(tile_data, index_row, axis=2))(per_tile_layout, sources)
    partials = jnp.einsum("tkqbc,tcd->tbkqd", picked, regrid, precision=lax.Precision.HIGHEST)
    destination_value = (atmos_tile_index.reshape(-1) * TILE_BLOCKS + atmos_block_index).astype(jnp.int32)
    accumulated_sum = jax.ops.segment_sum(partials.reshape(SECTION_TILES * REGRID_ENTRIES, WINDOW_STEPS, COUPLING_FIELDS, BLOCK_GRID_CELLS), destination_value,
                                 num_segments=SECTION_TILES * TILE_BLOCKS)
    accumulated_sum = accumulated_sum.reshape(N_GY, N_GX, TILE_BLOCKS, WINDOW_STEPS, COUPLING_FIELDS, BLOCK_GRID_CELLS).transpose(0, 1, 3, 4, 2, 5)
    accumulated_sum = accumulated_sum.reshape(N_GY, N_GX, WINDOW_STEPS, COUPLING_FIELDS, CY, CX).transpose(2, 3, 0, 4, 1, 5)
    return accumulated_sum.reshape(WINDOW_STEPS, COUPLING_FIELDS, NY, NX)


def reference(adjoint_init, diffusivity, mixing, coupling, history, extract, land_mask,
              regrid, atmos_tile_index, ocean_block_index, atmos_block_index):
    wet_mask = land_mask.astype(jnp.float32)
    ocean = adjoint_init[0]
    surfaces = [None] * WINDOW_STEPS
    for time_step in range(WINDOW_STEPS - 1, -1, -1):
        forcing = jnp.concatenate([history[0, time_step], history[1, time_step]], axis=0)
        ocean = advance(ocean, wet_mask, diffusivity[0], mixing[0], coupling[0], forcing)
        surfaces[time_step] = jnp.einsum("qc,cyx->qyx", extract, wet_mask * ocean,
                                         precision=lax.Precision.HIGHEST)
    received = regrid_surface(jnp.stack(surfaces), regrid, atmos_tile_index, ocean_block_index, atmos_block_index)
    atmos = adjoint_init[1]
    for time_step in range(WINDOW_STEPS - 1, -1, -1):
        forcing = jnp.concatenate([history[1, time_step], received[time_step]], axis=0)
        atmos = advance(atmos, 1.0, diffusivity[1], mixing[1], coupling[1], forcing)
    return jnp.stack([ocean, atmos])
```

```python
import functools

import jax
import jax.numpy as jnp
from jax import lax
from jax.experimental import pallas as pl
from jax.experimental.pallas import tpu as pltpu
from jax.sharding import PartitionSpec as P

MESH = pl.DeviceIdType.MESH
F32, BF16 = jnp.float32, jnp.bfloat16
NC, NY, NX = 32, 32, 256
STEPS, FIELDS = 4, 4
SUB = 8
BANDS = NY // SUB
CELLS = 128
BLOCKS = NY * NX // CELLS
CAP = 2
NT = (((1,), (1,)), ((), ()))


def iota(shape, axis):
    return lax.broadcasted_iota(jnp.int32, shape, axis)


def split(x):
    hi = x.astype(BF16)
    return hi, (x - hi.astype(F32)).astype(BF16)


def mm(a, b):
    return jnp.dot(a, b, preferred_element_type=F32)


def mm_nt(a, b):
    return lax.dot_general(a, b, NT, preferred_element_type=F32)


def onehot(cond):
    return jnp.where(cond, 1.0, 0.0).astype(BF16)


def widen(small):
    rows, columns = small.shape
    left = onehot(iota((rows * SUB, rows), 0) // SUB == iota((rows * SUB, rows), 1))
    right = onehot(iota((columns, columns * SUB), 1) // SUB == iota((columns, columns * SUB), 0))
    big = (rows * SUB, columns * SUB)
    same = iota(big, 0) % SUB == iota(big, 1) % SUB
    return [
        jnp.where(same, mm(mm(left, part).astype(BF16), right), 0.0).astype(BF16)
        for part in split(small)
    ]


def block_place(block):
    return (block % 2) * NY + block // 2


def kernel(
    n_gy, n_gx,
    adj_hbm, dif_hbm, mix_hbm, cou_hbm, his_hbm, ext_hbm, msk_hbm, reg_hbm, dst_hbm, src_hbm, blk_hbm,
    out_hbm,
    mix_ref, cou_ref, ext_ref, reg_ref, dst_ref, src_ref, blk_ref,
    state, wet, dif, hist, far, vee, acc, u_hi, u_lo, k_hi, k_lo, c_own, c_far, e_hi, e_lo, r_hi, r_lo,
    pick, place, packed, arrived, row_out, row_in, col_out, col_in,
    load_sem, far_send, far_recv, halo_send, halo_recv, a2a_send, a2a_recv, out_sem,
):
    sect, gy, gx = lax.axis_index("sect"), lax.axis_index("gy"), lax.axis_index("gx")
    tiles = n_gy * n_gx
    me = gy * n_gx + gx
    is_ocean, is_atmos = sect == 0, sect == 1
    west, east = lax.rem(gx + n_gx - 1, n_gx), lax.rem(gx + 1, n_gx)
    has_north, has_south = gy > 0, gy < n_gy - 1
    barrier = pltpu.get_barrier_semaphore()

    loads = [
        pltpu.make_async_copy(source, target, load_sem.at[j])
        for j, (source, target) in enumerate(
            (
                (mix_hbm.at[0], mix_ref), (cou_hbm.at[0], cou_ref), (ext_hbm, ext_ref), (dst_hbm, dst_ref),
                (src_hbm, src_ref), (blk_hbm, blk_ref), (reg_hbm.at[0], reg_ref), (dif_hbm.at[0], dif),
                (msk_hbm, wet), (adj_hbm.at[0], state), (his_hbm.at[0], hist),
            )
        )
    ]
    for load in loads:
        load.start()

    def signal(s, y, x):
        pl.semaphore_signal(barrier, inc=1, device_id=(s, y, x), device_id_type=MESH)

    @pl.when(gy == 0)
    def _():
        row_in[:, 0] = jnp.zeros_like(row_in[:, 0])

    @pl.when(gy == n_gy - 1)
    def _():
        row_in[:, 1] = jnp.zeros_like(row_in[:, 1])

    signal(sect, gy, west)
    signal(sect, gy, east)

    @pl.when(has_north)
    def _():
        signal(sect, gy - 1, gx)

    @pl.when(has_south)
    def _():
        signal(sect, gy + 1, gx)

    @pl.when(is_ocean)
    def _():
        signal(1, gy, gx)

    @pl.when(is_atmos)
    def _():
        def one(t, carry):
            signal(0, lax.rem(gy + t // n_gx, n_gy), lax.rem(gx + t % n_gx, n_gx))
            return carry

        lax.fori_loop(0, tiles, one, 0)

    for load in loads[:-1]:
        load.wait()

    k_hi[...], k_lo[...] = widen(mix_ref[...].T)
    for column, ref in ((0, c_own), (FIELDS, c_far)):
        hi, lo = widen(cou_ref[column : column + FIELDS, :].T)
        ref[...] = jnp.concatenate([hi, hi, lo], axis=1)

    @pl.when(is_ocean)
    def _():
        e_hi[...], e_lo[...] = widen(ext_ref[...])
        r_hi[...], r_lo[...] = split(reg_ref[...])
        entries = dst_ref.shape[1]
        dest = dst_ref[pl.ds(me, 1), :]
        source = block_place(src_ref[pl.ds(me, 1), :])
        dest_row = jnp.broadcast_to(dest, (entries, entries))
        dest_col = dest_row.T
        square = (entries, entries)
        earlier = (dest_row == dest_col) & (iota(square, 0) < iota(square, 1))
        rank = jnp.sum(jnp.where(earlier, 1, 0), axis=0, keepdims=True)
        position = dest * CAP + rank
        slots = tiles * CAP * FIELDS
        goes = onehot(jnp.broadcast_to(position, (slots, entries)) == iota((slots, entries), 0) // FIELDS)
        wide = FIELDS * BLOCKS
        reads = onehot(jnp.broadcast_to(source, (wide, entries)) == iota((wide, entries), 0) % BLOCKS)
        field = iota((slots, wide), 0) % FIELDS == iota((slots, wide), 1) // BLOCKS
        pick[...] = jnp.where(field, mm_nt(goes, reads), 0.0).astype(BF16)

    @pl.when(is_atmos)
    def _():
        entries = dst_ref.shape[1]
        square = (entries, entries)
        match = dst_ref[...] == me
        before = onehot(iota(square, 0) < iota(square, 1))
        rank = mm(onehot(match), before)
        block = (block_place(blk_ref[...]) + 1).astype(F32)
        slots = tiles * CAP * FIELDS
        spread = onehot(iota((tiles, slots), 1) // (CAP * FIELDS) == iota((tiles, slots), 0))
        which = (iota((SUB, slots), 1) // FIELDS) % CAP
        code = jnp.zeros((SUB, slots), F32)
        for r in range(CAP):
            value = jnp.where(match & (rank == r), block, 0.0).astype(BF16)
            row = mm_nt(jnp.ones((SUB, entries), BF16), value)
            code = jnp.where(which == r, mm(row.astype(BF16), spread), code)
        wide = FIELDS * BLOCKS
        shape = (wide, slots)
        lands = jnp.broadcast_to(code[:1], shape) == (iota(shape, 0) % BLOCKS + 1).astype(F32)
        field = iota(shape, 0) // BLOCKS == iota(shape, 1) % FIELDS
        place[...] = onehot(lands & field)

    def columns_packed():
        lane = iota((NY, CELLS), 1)
        rim = jnp.zeros((NY, CELLS), F32)
        for c in range(NC):
            rim = jnp.where(lane == c, pltpu.roll(vee[c, :, NX - CELLS :], c + 1, 1), rim)
            rim = jnp.where(lane == NC + c, pltpu.roll(vee[c, :, :CELLS], NC + c, 1), rim)
        return rim

    def halo_copies(i):
        def copy(j, source, target, y, x):
            return pltpu.make_async_remote_copy(
                src_ref=source, dst_ref=target, send_sem=halo_send.at[i, j], recv_sem=halo_recv.at[i, j],
                device_id=(sect, y, x), device_id_type=MESH,
            )

        return (
            copy(0, col_out.at[i], col_in.at[i, 0], gy, east),
            copy(1, col_out.at[i], col_in.at[i, 1], gy, west),
            copy(2, row_out.at[i, 1], row_in.at[i, 0], gy + 1, gx),
            copy(3, row_out.at[i, 0], row_in.at[i, 1], gy - 1, gx),
        )

    def prepare():
        for b in range(BANDS):
            rows = slice(b * SUB, (b + 1) * SUB)
            u = state[:, rows, :] * wet_f(rows)
            vee[:, rows, :] = u * dif[rows, :][None]
            u_hi[b], u_lo[b] = split(u.reshape(NC * SUB, NX))

    def wet_f(rows):
        return jnp.where(is_ocean, wet[rows, :].astype(F32), 1.0)[None]

    def rim_out(i):
        col_out[i] = columns_packed()
        for c in range(NC):
            row_out[i, 0, c : c + 1, :] = vee[c, :1, :]
            row_out[i, 1, c : c + 1, :] = vee[c, NY - 1 :, :]

    def rim_send(i):
        e, w, s, n = halo_copies(i)
        e.start()
        w.start()

        @pl.when(has_south)
        def _():
            s.start()

        @pl.when(has_north)
        def _():
            n.start()

    def rim_wait(i):
        e, w, s, n = halo_copies(i)
        e.wait()
        w.wait()

        @pl.when(has_south)
        def _():
            s.wait_send()
            n.wait_recv()

        @pl.when(has_north)
        def _():
            n.wait_send()
            s.wait_recv()

    def forced(coefs, fields):
        hi, lo = split(fields.reshape(FIELDS * SUB, NX))
        return mm(coefs[...], jnp.concatenate([hi, lo, hi], axis=0))

    def mix(k):
        for b in range(BANDS):
            rows = slice(b * SUB, (b + 1) * SUB)
            total = mm(k_hi[...], u_hi[b]) + mm(k_hi[...], u_lo[b]) + mm(k_lo[...], u_hi[b])
            total += forced(c_own, hist[k, :, rows, :])
            acc[:, rows, :] = total.reshape(NC, SUB, NX)

    def add_far(k, fields):
        for b in range(BANDS):
            rows = slice(b * SUB, (b + 1) * SUB)
            acc[:, rows, :] += forced(c_far, fields(rows)).reshape(NC, SUB, NX)

    def spread(i):
        row, lane = iota((NY, NX), 0), iota((NY, NX), 1)
        from_west, from_east = col_in[i, 0], col_in[i, 1]
        wet_all = jnp.where(is_ocean, wet[...].astype(F32), 1.0)
        for c in range(NC):
            v = vee[c]
            up = jnp.where(row == 0, jnp.broadcast_to(row_in[i, 0, c : c + 1, :], (NY, NX)), pltpu.roll(v, 1, 0))
            down = jnp.where(
                row == NY - 1, jnp.broadcast_to(row_in[i, 1, c : c + 1, :], (NY, NX)), pltpu.roll(v, NY - 1, 0)
            )
            left = jnp.where(
                lane == 0, jnp.broadcast_to(from_west[:, c : c + 1], (NY, NX)), pltpu.roll(v, 1, 1)
            )
            right = jnp.where(
                lane == NX - 1,
                jnp.broadcast_to(from_east[:, NC + c : NC + c + 1], (NY, NX)),
                pltpu.roll(v, NX - 1, 1),
            )
            state[c] = acc[c] + wet_all * state[c] + (((up + down) + (left + right)) - 4.0 * v)

    def deliver(k):
        surface = []
        for b in range(BANDS):
            surface.append(
                mm(e_hi[...], u_hi[b]) + mm(e_hi[...], u_lo[b]) + mm(e_lo[...], u_hi[b])
            )
        parts = [
            surface[b][q * SUB : (q + 1) * SUB, h * CELLS : (h + 1) * CELLS]
            for q in range(FIELDS) for h in range(2) for b in range(BANDS)
        ]
        hi, lo = split(jnp.concatenate(parts, axis=0))
        regridded = mm(hi, r_hi[...]) + mm(lo, r_hi[...]) + mm(hi, r_lo[...])
        hi, lo = split(regridded)
        slots = mm(pick[...], hi) + mm(pick[...], lo)
        packed[k] = slots.reshape(tiles, CAP * FIELDS, CELLS)

        def one(t, carry):
            y, x = lax.rem(gy + t // n_gx, n_gy), lax.rem(gx + t % n_gx, n_gx)
            pltpu.make_async_remote_copy(
                src_ref=packed.at[k, y * n_gx + x], dst_ref=arrived.at[k, me],
                send_sem=a2a_send.at[k], recv_sem=a2a_recv.at[k],
                device_id=(1, y, x), device_id_type=MESH,
            ).start()
            return carry

        lax.fori_loop(0, tiles, one, 0)

    def receive(k):
        pltpu.make_async_copy(arrived.at[k], arrived.at[k], a2a_recv.at[k]).wait()
        hi, lo = split(arrived[k].reshape(tiles * CAP * FIELDS, CELLS))
        sums = mm(place[...], hi) + mm(place[...], lo)
        for q in range(FIELDS):
            for h in range(2):
                start = (q * 2 + h) * NY
                far[k, q, :, h * CELLS : (h + 1) * CELLS] = sums[start : start + NY]
        for b in range(BANDS):
            rows = slice(b * SUB, (b + 1) * SUB)
            state[:, rows, :] += forced(c_far, far[k, :, rows, :]).reshape(NC, SUB, NX)

    def far_copy(k, target_sect):
        return pltpu.make_async_remote_copy(
            src_ref=his_hbm.at[0, k], dst_ref=far.at[k], send_sem=far_send.at[k], recv_sem=far_recv.at[k],
            device_id=(target_sect, gy, gx), device_id_type=MESH,
        )

    prepare()
    rim_out(0)

    peers = jnp.where(is_ocean, tiles, 1) + 2 + jnp.where(has_north, 1, 0) + jnp.where(has_south, 1, 0)
    pl.semaphore_wait(barrier, peers)
    rim_send(0)

    @pl.when(is_atmos)
    def _():
        for k in range(STEPS - 1, -1, -1):
            far_copy(k, 0).start()

    loads[-1].wait()

    def step(i, carry):
        k = STEPS - 1 - i
        mix(k)

        @pl.when(is_ocean)
        def _():
            far_copy(k, 1).wait_recv()
            add_far(k, lambda rows: far[k, :, rows, :])

        rim_wait(i)
        spread(i)

        @pl.when(is_atmos)
        def _():
            receive(k)

        @pl.when(i < STEPS - 1)
        def _():
            prepare()
            rim_out(i + 1)
            rim_send(i + 1)

        @pl.when(is_ocean)
        def _():
            @pl.when(i == STEPS - 1)
            def _():
                prepare()

            deliver(k)

        return carry

    lax.fori_loop(0, STEPS, step, 0)
    out = pltpu.make_async_copy(state, out_hbm.at[0], out_sem)
    out.start()

    @pl.when(is_ocean)
    def _():
        for k in range(STEPS):
            pltpu.make_async_copy(packed.at[k], packed.at[k], a2a_send.at[k]).wait()

    @pl.when(is_atmos)
    def _():
        for k in range(STEPS):
            far_copy(k, 0).wait_send()

    out.wait()


def body(n_gy, n_gx, adj, dif, mix, cou, his, ext, msk, reg, dst, src, blk):
    tiles = n_gy * n_gx
    entries = src.shape[0] // tiles
    tables = [x.reshape(tiles, entries) for x in (dst, src, blk)]
    anywhere = pl.BlockSpec(memory_space=pl.ANY)
    rows, slots, wide = NC * SUB, tiles * CAP * FIELDS, FIELDS * BLOCKS
    dma = pltpu.SemaphoreType.DMA
    return pl.pallas_call(
        functools.partial(kernel, n_gy, n_gx),
        out_shape=jax.ShapeDtypeStruct(adj.shape, F32),
        in_specs=[anywhere] * 11,
        out_specs=anywhere,
        scratch_shapes=[
            pltpu.VMEM((NC, NC), F32),
            pltpu.VMEM((2 * FIELDS, NC), F32),
            pltpu.VMEM((FIELDS, NC), F32),
            pltpu.VMEM((CELLS, CELLS), F32),
            pltpu.VMEM((tiles, entries), jnp.int32),
            pltpu.VMEM((tiles, entries), jnp.int32),
            pltpu.VMEM((tiles, entries), jnp.int32),
            pltpu.VMEM((NC, NY, NX), F32),
            pltpu.VMEM((NY, NX), jnp.int32),
            pltpu.VMEM((NY, NX), F32),
            pltpu.VMEM((STEPS, FIELDS, NY, NX), F32),
            pltpu.VMEM((STEPS, FIELDS, NY, NX), F32),
            pltpu.VMEM((NC, NY, NX), F32),
            pltpu.VMEM((NC, NY, NX), F32),
            pltpu.VMEM((BANDS, rows, NX), BF16),
            pltpu.VMEM((BANDS, rows, NX), BF16),
            pltpu.VMEM((rows, rows), BF16),
            pltpu.VMEM((rows, rows), BF16),
            pltpu.VMEM((rows, 3 * FIELDS * SUB), BF16),
            pltpu.VMEM((rows, 3 * FIELDS * SUB), BF16),
            pltpu.VMEM((FIELDS * SUB, rows), BF16),
            pltpu.VMEM((FIELDS * SUB, rows), BF16),
            pltpu.VMEM((CELLS, CELLS), BF16),
            pltpu.VMEM((CELLS, CELLS), BF16),
            pltpu.VMEM((slots, wide), BF16),
            pltpu.VMEM((wide, slots), BF16),
            pltpu.VMEM((STEPS, tiles, CAP * FIELDS, CELLS), F32),
            pltpu.VMEM((STEPS, tiles, CAP * FIELDS, CELLS), F32),
            pltpu.VMEM((STEPS, 2, NC, NX), F32),
            pltpu.VMEM((STEPS, 2, NC, NX), F32),
            pltpu.VMEM((STEPS, NY, CELLS), F32),
            pltpu.VMEM((STEPS, 2, NY, CELLS), F32),
            dma((11,)), dma((STEPS,)), dma((STEPS,)), dma((STEPS, 4)), dma((STEPS, 4)),
            dma((STEPS,)), dma((STEPS,)), dma,
        ],
        compiler_params=pltpu.CompilerParams(
            collective_id=0, has_side_effects=True, vmem_limit_bytes=67043328
        ),
    )(adj, dif, mix, cou.swapaxes(1, 2), his, ext, msk, reg, *tables)


def solution(mesh):
    placed = (
        P("sect", None, "gy", "gx"), P("sect", "gy", "gx"), P("sect", None, None), P("sect", None, None),
        P("sect", None, None, "gy", "gx"), P(), P("gy", "gx"), P(("gy", "gx"), None, None), P(), P(), P(),
    )
    return jax.shard_map(
        functools.partial(body, mesh.shape["gy"], mesh.shape["gx"]),
        mesh=mesh, in_specs=placed, out_specs=P("sect", None, "gy", "gx"), check_vma=False,
    )
```

```python
import functools
import itertools
import math

import jax
import jax.numpy as jnp
from jax import lax
from jax.experimental import pallas as pl
from jax.experimental.pallas import tpu as pltpu
from jax.sharding import PartitionSpec as P

MESH = pl.DeviceIdType.MESH
F32, BF16 = jnp.float32, jnp.bfloat16
NC, NY, NX = 32, 32, 256
STEPS, FIELDS = 4, 4
SUB = 8
BANDS = NY // SUB
CELLS = 128
BLOCKS = NY * NX // CELLS
CAP = 2
NT = (((1,), (1,)), ((), ()))


def iota(shape, axis):
    return lax.broadcasted_iota(jnp.int32, shape, axis)


def split(x):
    hi = x.astype(BF16)
    return hi, (x - hi.astype(F32)).astype(BF16)


def mm(a, b):
    return jnp.dot(a, b, preferred_element_type=F32)


def mm_nt(a, b):
    return lax.dot_general(a, b, NT, preferred_element_type=F32)


def onehot(cond):
    return jnp.where(cond, 1.0, 0.0).astype(BF16)


def widen(small):
    rows, columns = small.shape
    left = onehot(iota((rows * SUB, rows), 0) // SUB == iota((rows * SUB, rows), 1))
    right = onehot(iota((columns, columns * SUB), 1) // SUB == iota((columns, columns * SUB), 0))
    big = (rows * SUB, columns * SUB)
    same = iota(big, 0) % SUB == iota(big, 1) % SUB
    return [
        jnp.where(same, mm(mm(left, part).astype(BF16), right), 0.0).astype(BF16)
        for part in split(small)
    ]


def block_place(block):
    return (block % 2) * NY + block // 2


def kernel(
    n_gy, n_gx,
    adj_hbm, dif_hbm, mix_hbm, cou_hbm, his_hbm, ext_hbm, msk_hbm, reg_hbm, dst_hbm, src_hbm, blk_hbm,
    out_ref,
    mix_ref, cou_ref, ext_ref, reg_ref, dst_ref, src_ref, blk_ref,
    wet, dif, hist, far, vee, acc, u_hi, u_lo, k_hi, k_lo, c_own, c_far, e_hi, e_lo, r_hi, r_lo,
    pick, place, packed, arrived, row_out, row_in, col_out, col_in,
    late, late_vee, late_row_out, late_row_in, late_col_out, late_col_in,
    load_sem, ready, far_send, far_recv, halo_send, halo_recv, a2a_send, a2a_recv, late_send, late_recv,
):
    sect, gy, gx = lax.axis_index("sect"), lax.axis_index("gy"), lax.axis_index("gx")
    tiles = n_gy * n_gx
    me = gy * n_gx + gx
    is_ocean, is_atmos = sect == 0, sect == 1
    west, east = lax.rem(gx + n_gx - 1, n_gx), lax.rem(gx + 1, n_gx)
    side = math.isqrt(n_gy)

    def farthest_first():
        def hops(offset):
            return sum(min(d, n - d) for d, n in zip(offset, (side, side, n_gx)))

        along_x = [lax.rem(gy // side + t, side) * side for t in range(side)]
        along_y = [lax.rem(lax.rem(gy, side) + t, side) for t in range(side)]
        along_z = [lax.rem(gx + t, n_gx) for t in range(n_gx)]
        offsets = itertools.product(range(side), range(side), range(n_gx))
        return [(along_x[i] + along_y[j], along_z[l]) for i, j, l in sorted(offsets, key=hops, reverse=True)]

    has_north, has_south = gy > 0, gy < n_gy - 1
    barrier = pltpu.get_barrier_semaphore()
    state = out_ref.at[0]

    loads = [
        pltpu.make_async_copy(source, target, load_sem.at[j])
        for j, (source, target) in enumerate(
            (
                (adj_hbm.at[0], state), (dif_hbm.at[0], dif), (msk_hbm, wet), (mix_hbm.at[0], mix_ref),
                (cou_hbm.at[0], cou_ref), (ext_hbm, ext_ref), (dst_hbm, dst_ref), (src_hbm, src_ref),
                (blk_hbm, blk_ref), (reg_hbm.at[0], reg_ref), (his_hbm.at[0], hist),
            )
        )
    ]
    for load in loads:
        load.start()

    def signal(s, y, x):
        pl.semaphore_signal(barrier, inc=1, device_id=(s, y, x), device_id_type=MESH)

    @pl.when(gy == 0)
    def _():
        for ref in (row_in, late_row_in):
            ref[:, 0] = jnp.zeros_like(ref[:, 0])

    @pl.when(gy == n_gy - 1)
    def _():
        for ref in (row_in, late_row_in):
            ref[:, 1] = jnp.zeros_like(ref[:, 1])

    signal(sect, gy, west)
    signal(sect, gy, east)

    @pl.when(is_ocean)
    def _():
        for t in range(1, n_gy):
            signal(0, lax.rem(gy + t, n_gy), gx)
        signal(1, gy, gx)

    @pl.when(is_atmos)
    def _():
        for t in range(n_gx):
            signal(0, gy, lax.rem(gx + t, n_gx))

        @pl.when(has_north)
        def _():
            signal(1, gy - 1, gx)

        @pl.when(has_south)
        def _():
            signal(1, gy + 1, gx)

    def halo_copies(i):
        return rim_copies(i, col_out, col_in, row_out, row_in, halo_send, halo_recv)

    def rim_copies(i, col_out, col_in, row_out, row_in, halo_send, halo_recv):
        def copy(j, source, target, y, x):
            return pltpu.make_async_remote_copy(
                src_ref=source, dst_ref=target, send_sem=halo_send.at[i, j], recv_sem=halo_recv.at[i, j],
                device_id=(sect, y, x), device_id_type=MESH,
            )

        return (
            copy(0, col_out.at[i, 0], col_in.at[i, 0], gy, east),
            copy(1, col_out.at[i, 1], col_in.at[i, 1], gy, west),
            copy(2, row_out.at[i, 1], row_in.at[i, 0], gy + 1, gx),
            copy(3, row_out.at[i, 0], row_in.at[i, 1], gy - 1, gx),
        )

    def prepare():
        for b in range(BANDS):
            rows = slice(b * SUB, (b + 1) * SUB)
            u = state[:, rows, :] * wet_f(rows)
            vee[:, rows, :] = u * dif[rows, :][None]
            u_hi[b], u_lo[b] = split(u.reshape(NC * SUB, NX))

    def wet_f(rows):
        return jnp.where(is_ocean, wet[rows, :].astype(F32), 1.0)[None]

    def rim_out(i):
        rim_pack(i, vee, NC, col_out, row_out)

    def rim_pack(i, vee, count, col_out, row_out):
        lane = iota((SUB, CELLS), 1)
        east_rim, west_rim = jnp.zeros((SUB, CELLS), F32), jnp.zeros((SUB, CELLS), F32)
        for c in range(count):
            row_out[i, 0, c : c + 1, :] = vee[c, :1, :]
            row_out[i, 1, c : c + 1, :] = vee[c, NY - 1 :, :]
            for b in range(BANDS):
                rows, at = slice(b * SUB, (b + 1) * SUB), b * NC + c
                east_rim = jnp.where(
                    lane == at, pltpu.roll(vee[c, rows, NX - CELLS :], (at + 1) % CELLS, 1), east_rim
                )
                west_rim = jnp.where(lane == at, pltpu.roll(vee[c, rows, :CELLS], at, 1) if at else vee[c, rows, :CELLS], west_rim)
        col_out[i, 0], col_out[i, 1] = east_rim, west_rim

    def rim_send(i, copies=halo_copies):
        e, w, s, n = copies(i)
        e.start()
        w.start()

        @pl.when(has_south)
        def _():
            s.start()

        @pl.when(has_north)
        def _():
            n.start()

    def rim_wait(i, copies=halo_copies):
        e, w, s, n = copies(i)
        e.wait()
        w.wait()

        @pl.when(has_south)
        def _():
            s.wait_send()
            n.wait_recv()

        @pl.when(has_north)
        def _():
            n.wait_send()
            s.wait_recv()

    def forced(coefs, fields):
        hi, lo = split(fields.reshape(FIELDS * SUB, NX))
        return mm(coefs, jnp.concatenate([hi, lo, hi], axis=0))

    def mix(k):
        for b in range(BANDS):
            rows = slice(b * SUB, (b + 1) * SUB)
            total = mm(k_hi[...], u_hi[b]) + mm(k_hi[...], u_lo[b]) + mm(k_lo[...], u_hi[b])
            total += forced(c_own[...], hist[k, :, rows, :])
            acc[:, rows, :] = total.reshape(NC, SUB, NX)

    def add_far(target, j, fields):
        for b in range(BANDS):
            rows = slice(b * SUB, (b + 1) * SUB)
            target[:, rows, :] += forced(c_far[j], fields[:, rows, :]).reshape(NC, SUB, NX)

    def laplace(i, c, vee, col_in, row_in):
        row, lane = iota((NY, NX), 0), iota((NY, NX), 1)
        v = vee[c]
        north, south = row_in[i, 0, c : c + 1, :], row_in[i, 1, c : c + 1, :]
        whole = (NY, NX)

        def column(j):
            bands = [col_in[i, j, :, b * NC + c : b * NC + c + 1] for b in range(BANDS)]
            return jnp.concatenate([jnp.broadcast_to(x, (SUB, CELLS)) for x in bands], axis=0)

        from_west, from_east = column(0), column(1)
        up = jnp.where(row == 0, jnp.broadcast_to(north, whole), pltpu.roll(v, 1, 0))
        down = jnp.where(row == NY - 1, jnp.broadcast_to(south, whole), pltpu.roll(v, NY - 1, 0))
        left = jnp.where(lane == 0, jnp.concatenate([from_west] * 2, axis=1), pltpu.roll(v, 1, 1))
        right = jnp.where(lane == NX - 1, jnp.concatenate([from_east] * 2, axis=1), pltpu.roll(v, NX - 1, 1))
        return ((up + down) + (left + right)) - 4.0 * v

    def spread(i):
        wet_all = jnp.where(is_ocean, wet[...].astype(F32), 1.0)
        for c in range(NC):
            state[c] = acc[c] + wet_all * state[c] + laplace(i, c, vee, col_in, row_in)

    def deliver(k):
        surface = []
        for b in range(BANDS):
            surface.append(
                mm(e_hi[...], u_hi[b]) + mm(e_hi[...], u_lo[b]) + mm(e_lo[...], u_hi[b])
            )
        parts = [
            surface[b][q * SUB : (q + 1) * SUB, h * CELLS : (h + 1) * CELLS]
            for q in range(FIELDS) for h in range(2) for b in range(BANDS)
        ]
        hi, lo = split(jnp.concatenate(parts, axis=0))
        regridded = mm(hi, r_hi[...]) + mm(lo, r_hi[...]) + mm(hi, r_lo[...])
        hi, lo = split(regridded)
        slots = mm(pick[...], hi) + mm(pick[...], lo)
        packed[k] = slots.reshape(tiles, CAP * FIELDS, CELLS)

        for y, x in farthest_first():
            pltpu.make_async_remote_copy(
                src_ref=packed.at[k, y * n_gx + x], dst_ref=arrived.at[k, me],
                send_sem=a2a_send.at[k], recv_sem=a2a_recv.at[k],
                device_id=(1, y, x), device_id_type=MESH,
            ).start()

    def receive(k):
        pltpu.make_async_copy(arrived.at[k], arrived.at[k], a2a_recv.at[k]).wait()
        hi, lo = split(arrived[k].reshape(tiles * CAP * FIELDS, CELLS))
        sums = mm(place[...], hi) + mm(place[...], lo)
        for q in range(FIELDS):
            for h in range(2):
                start = (q * 2 + h) * NY
                far[k, q, :, h * CELLS : (h + 1) * CELLS] = sums[start : start + NY]

    def late_copies(n):
        return rim_copies(n, late_col_out, late_col_in, late_row_out, late_row_in, late_send, late_recv)

    def late_start(n, fields):
        for j, field in enumerate(fields):
            for q in range(FIELDS):
                late_vee[j * FIELDS + q] = field[q] * dif[...]
        rim_pack(n, late_vee, len(fields) * FIELDS, late_col_out, late_row_out)
        rim_send(n, late_copies)

    def late_end(n, outputs):
        rim_wait(n, late_copies)
        for j, (ref, q_of) in enumerate(outputs):
            for q in range(FIELDS):
                ref[q] = q_of(laplace(n, j * FIELDS + q, late_vee, late_col_in, late_row_in), q)

    def atmosphere_end():
        first, second = late.at[0], late.at[1]
        receive(3)
        late_start(0, [far.at[3]])
        add_far(state, 3, far.at[3])
        late_end(0, [(first, lambda x, q: x)])
        receive(2)
        for q in range(FIELDS):
            x, r = first[q], far[2, q]
            first[q] = x + r
            second[q] = 3.0 * x + 2.0 * r
            far[3, q] = 3.0 * x + r
        late_start(1, [first, second])
        add_far(state, 2, far.at[3])
        late_end(1, [(first, lambda x, q: x), (second, lambda x, q: x)])
        receive(1)
        for q in range(FIELDS):
            r = far[1, q]
            first[q] += r
            second[q] += r
        late_start(2, [first])
        add_far(state, 1, second)
        late_end(2, [(first, lambda x, q: x)])
        receive(0)
        for q in range(FIELDS):
            first[q] += far[0, q]
        add_far(state, 0, first)

    def far_copy(k, target_sect):
        return pltpu.make_async_remote_copy(
            src_ref=his_hbm.at[0, k], dst_ref=far.at[k], send_sem=far_send.at[k], recv_sem=far_recv.at[k],
            device_id=(target_sect, gy, gx), device_id_type=MESH,
        )

    for load in loads[:3]:
        load.wait()
    prepare()
    rim_out(0)

    beside = jnp.where(has_north, 1, 0) + jnp.where(has_south, 1, 0)
    pl.semaphore_wait(barrier, 2 + jnp.where(is_ocean, n_gx + n_gy - 1, 1 + beside))
    rim_send(0)

    @pl.when(is_ocean)
    def _():
        for t in range(1, n_gy):
            pl.semaphore_signal(
                ready, inc=1, device_id=(0, lax.rem(gy + t, n_gy), gx), device_id_type=MESH
            )

    @pl.when(is_atmos)
    def _():
        for k in range(STEPS - 1, -1, -1):
            far_copy(k, 0).start()

    for load in loads[3:]:
        load.wait()

    k_hi[...], k_lo[...] = widen(mix_ref[...].T)

    def triple(small):
        hi, lo = widen(small)
        return jnp.concatenate([hi, hi, lo], axis=1)

    c_own[...] = triple(cou_ref[:FIELDS, :].T)
    c_far[0] = triple(cou_ref[FIELDS:, :].T)

    @pl.when(is_ocean)
    def _():
        e_hi[...], e_lo[...] = widen(ext_ref[...])
        r_hi[...], r_lo[...] = split(reg_ref[...])
        entries = dst_ref.shape[1]
        dest = dst_ref[pl.ds(me, 1), :]
        source = block_place(src_ref[pl.ds(me, 1), :])
        dest_row = jnp.broadcast_to(dest, (entries, entries))
        dest_col = dest_row.T
        square = (entries, entries)
        earlier = (dest_row == dest_col) & (iota(square, 0) < iota(square, 1))
        rank = jnp.sum(jnp.where(earlier, 1, 0), axis=0, keepdims=True)
        position = dest * CAP + rank
        slots = tiles * CAP * FIELDS
        goes = onehot(jnp.broadcast_to(position, (slots, entries)) == iota((slots, entries), 0) // FIELDS)
        wide = FIELDS * BLOCKS
        reads = onehot(jnp.broadcast_to(source, (wide, entries)) == iota((wide, entries), 0) % BLOCKS)
        field = iota((slots, wide), 0) % FIELDS == iota((slots, wide), 1) // BLOCKS
        pick[...] = jnp.where(field, mm_nt(goes, reads), 0.0).astype(BF16)

    @pl.when(is_atmos)
    def _():
        entries = dst_ref.shape[1]
        square = (entries, entries)
        match = dst_ref[...] == me
        before = onehot(iota(square, 0) < iota(square, 1))
        rank = mm(onehot(match), before)
        block = (block_place(blk_ref[...]) + 1).astype(F32)
        slots = tiles * CAP * FIELDS
        spread = onehot(iota((tiles, slots), 1) // (CAP * FIELDS) == iota((tiles, slots), 0))
        which = (iota((SUB, slots), 1) // FIELDS) % CAP
        code = jnp.zeros((SUB, slots), F32)
        for r in range(CAP):
            value = jnp.where(match & (rank == r), block, 0.0).astype(BF16)
            row = mm_nt(jnp.ones((SUB, entries), BF16), value)
            code = jnp.where(which == r, mm(row.astype(BF16), spread), code)
        wide = FIELDS * BLOCKS
        shape = (wide, slots)
        lands = jnp.broadcast_to(code[:1], shape) == (iota(shape, 0) % BLOCKS + 1).astype(F32)
        field = iota(shape, 0) // BLOCKS == iota(shape, 1) % FIELDS
        place[...] = onehot(lands & field)
        mixed = cou_ref[FIELDS:, :].T
        for j in range(1, STEPS):
            mixed += jnp.dot(
                mix_ref[...].T, mixed, precision=lax.Precision.HIGHEST, preferred_element_type=F32
            )
            c_far[j] = triple(mixed)

    def step(i, carry):
        k = STEPS - 1 - i
        mix(k)

        @pl.when(is_ocean)
        def _():
            far_copy(k, 1).wait_recv()
            add_far(acc, 0, far.at[k])

        rim_wait(i)
        spread(i)

        @pl.when(i < STEPS - 1)
        def _():
            prepare()
            rim_out(i + 1)
            rim_send(i + 1)

        @pl.when(is_ocean)
        def _():
            @pl.when(i == STEPS - 1)
            def _():
                prepare()

            @pl.when(i == 0)
            def _():
                pl.semaphore_wait(ready, n_gy - 1)

            deliver(k)

        return carry

    lax.fori_loop(0, STEPS, step, 0)

    @pl.when(is_atmos)
    def _():
        atmosphere_end()

    @pl.when(is_ocean)
    def _():
        for k in range(STEPS):
            pltpu.make_async_copy(packed.at[k], packed.at[k], a2a_send.at[k]).wait()

    @pl.when(is_atmos)
    def _():
        for k in range(STEPS):
            far_copy(k, 0).wait_send()


def body(n_gy, n_gx, adj, dif, mix, cou, his, ext, msk, reg, dst, src, blk):
    tiles = n_gy * n_gx
    entries = src.shape[0] // tiles
    tables = [x.reshape(tiles, entries) for x in (dst, src, blk)]
    anywhere = pl.BlockSpec(memory_space=pl.ANY)
    rows, slots, wide = NC * SUB, tiles * CAP * FIELDS, FIELDS * BLOCKS
    dma = pltpu.SemaphoreType.DMA
    return pl.pallas_call(
        functools.partial(kernel, n_gy, n_gx),
        out_shape=pltpu.VMEM(adj.shape, F32),
        in_specs=[anywhere] * 11,
        out_specs=pl.BlockSpec(memory_space=pltpu.VMEM),
        scratch_shapes=[
            pltpu.VMEM((NC, NC), F32),
            pltpu.VMEM((2 * FIELDS, NC), F32),
            pltpu.VMEM((FIELDS, NC), F32),
            pltpu.VMEM((CELLS, CELLS), F32),
            pltpu.VMEM((tiles, entries), jnp.int32),
            pltpu.VMEM((tiles, entries), jnp.int32),
            pltpu.VMEM((tiles, entries), jnp.int32),
            pltpu.VMEM((NY, NX), jnp.int32),
            pltpu.VMEM((NY, NX), F32),
            pltpu.VMEM((STEPS, FIELDS, NY, NX), F32),
            pltpu.VMEM((STEPS, FIELDS, NY, NX), F32),
            pltpu.VMEM((NC, NY, NX), F32),
            pltpu.VMEM((NC, NY, NX), F32),
            pltpu.VMEM((BANDS, rows, NX), BF16),
            pltpu.VMEM((BANDS, rows, NX), BF16),
            pltpu.VMEM((rows, rows), BF16),
            pltpu.VMEM((rows, rows), BF16),
            pltpu.VMEM((rows, 3 * FIELDS * SUB), BF16),
            pltpu.VMEM((STEPS, rows, 3 * FIELDS * SUB), BF16),
            pltpu.VMEM((FIELDS * SUB, rows), BF16),
            pltpu.VMEM((FIELDS * SUB, rows), BF16),
            pltpu.VMEM((CELLS, CELLS), BF16),
            pltpu.VMEM((CELLS, CELLS), BF16),
            pltpu.VMEM((slots, wide), BF16),
            pltpu.VMEM((wide, slots), BF16),
            pltpu.VMEM((STEPS, tiles, CAP * FIELDS, CELLS), F32),
            pltpu.VMEM((STEPS, tiles, CAP * FIELDS, CELLS), F32),
            pltpu.VMEM((STEPS, 2, NC, NX), F32),
            pltpu.VMEM((STEPS, 2, NC, NX), F32),
            pltpu.VMEM((STEPS, 2, SUB, CELLS), F32),
            pltpu.VMEM((STEPS, 2, SUB, CELLS), F32),
            pltpu.VMEM((2, FIELDS, NY, NX), F32),
            pltpu.VMEM((2 * FIELDS, NY, NX), F32),
            pltpu.VMEM((STEPS - 1, 2, 2 * FIELDS, NX), F32),
            pltpu.VMEM((STEPS - 1, 2, 2 * FIELDS, NX), F32),
            pltpu.VMEM((STEPS - 1, 2, SUB, CELLS), F32),
            pltpu.VMEM((STEPS - 1, 2, SUB, CELLS), F32),
            dma((11,)), pltpu.SemaphoreType.REGULAR, dma((STEPS,)), dma((STEPS,)), dma((STEPS, 4)), dma((STEPS, 4)),
            dma((STEPS,)), dma((STEPS,)), dma((STEPS - 1, 4)), dma((STEPS - 1, 4)),
        ],
        compiler_params=pltpu.CompilerParams(
            collective_id=0, has_side_effects=True, vmem_limit_bytes=60 * 1024 * 1024
        ),
    )(adj, dif, mix, cou.swapaxes(1, 2), his, ext, msk, reg, *tables)


def solution(mesh):
    placed = (
        P("sect", None, "gy", "gx"), P("sect", "gy", "gx"), P("sect", None, None), P("sect", None, None),
        P("sect", None, None, "gy", "gx"), P(), P("gy", "gx"), P(("gy", "gx"), None, None), P(), P(), P(),
    )
    return jax.shard_map(
        functools.partial(body, mesh.shape["gy"], mesh.shape["gx"]),
        mesh=mesh, in_specs=placed, out_specs=P("sect", None, "gy", "gx"), check_vma=False,
    )
```

```python
import functools
import itertools
import math

import jax
import jax.numpy as jnp
from jax import lax
from jax.experimental import pallas as pl
from jax.experimental.pallas import tpu as pltpu
from jax.sharding import PartitionSpec as P

MESH = pl.DeviceIdType.MESH
F32, BF16 = jnp.float32, jnp.bfloat16
NC, NY, NX = 32, 32, 256
STEPS, FIELDS = 4, 4
SUB = 8
BANDS = NY // SUB
CELLS = 128
BLOCKS = NY * NX // CELLS
CAP = 2
NT = (((1,), (1,)), ((), ()))


def iota(shape, axis):
    return lax.broadcasted_iota(jnp.int32, shape, axis)


def split(x):
    hi = x.astype(BF16)
    return hi, (x - hi.astype(F32)).astype(BF16)


def mm(a, b):
    return jnp.dot(a, b, preferred_element_type=F32)


def mm_nt(a, b):
    return lax.dot_general(a, b, NT, preferred_element_type=F32)


def onehot(cond):
    return jnp.where(cond, 1.0, 0.0).astype(BF16)


def widen(small):
    rows, columns = small.shape
    left = onehot(iota((rows * SUB, rows), 0) // SUB == iota((rows * SUB, rows), 1))
    right = onehot(iota((columns, columns * SUB), 1) // SUB == iota((columns, columns * SUB), 0))
    big = (rows * SUB, columns * SUB)
    same = iota(big, 0) % SUB == iota(big, 1) % SUB
    return [
        jnp.where(same, mm(mm(left, part).astype(BF16), right), 0.0).astype(BF16)
        for part in split(small)
    ]


def block_place(block):
    return (block % 2) * NY + block // 2


def kernel(
    n_gy, n_gx,
    adj_hbm, dif_hbm, mix_hbm, cou_hbm, his_hbm, ext_hbm, msk_hbm, reg_hbm, dst_hbm, src_hbm, blk_hbm,
    out_ref,
    mix_ref, cou_ref, ext_ref, reg_ref, dst_ref, src_ref, blk_ref,
    wet, dif, hist, far, vee, acc, u_hi, u_lo, k_hi, k_lo, c_own, c_far, e_hi, e_lo, r_hi, r_lo,
    pick, place, packed, arrived, row_out, row_in, col_out, col_in,
    late, late_vee, late_row_out, late_row_in, late_col_out, late_col_in,
    load_sem, ready, far_send, far_recv, halo_send, halo_recv, a2a_send, a2a_recv, late_send, late_recv,
):
    sect, gy, gx = lax.axis_index("sect"), lax.axis_index("gy"), lax.axis_index("gx")
    tiles = n_gy * n_gx
    me = gy * n_gx + gx
    is_ocean, is_atmos = sect == 0, sect == 1
    west, east = lax.rem(gx + n_gx - 1, n_gx), lax.rem(gx + 1, n_gx)
    side = math.isqrt(n_gy)

    def farthest_first():
        def hops(offset):
            return sum(min(d, n - d) for d, n in zip(offset, (side, side, n_gx)))

        along_x = [lax.rem(gy // side + t, side) * side for t in range(side)]
        along_y = [lax.rem(lax.rem(gy, side) + t, side) for t in range(side)]
        along_z = [lax.rem(gx + t, n_gx) for t in range(n_gx)]
        offsets = itertools.product(range(side), range(side), range(n_gx))
        return [(along_x[i] + along_y[j], along_z[l]) for i, j, l in sorted(offsets, key=hops, reverse=True)]

    has_north, has_south = gy > 0, gy < n_gy - 1
    barrier = pltpu.get_barrier_semaphore()
    state = out_ref.at[0]

    loads = [
        pltpu.make_async_copy(source, target, load_sem.at[j])
        for j, (source, target) in enumerate(
            (
                (adj_hbm.at[0], state), (dif_hbm.at[0], dif), (msk_hbm, wet), (mix_hbm.at[0], mix_ref),
                (cou_hbm.at[0], cou_ref), (ext_hbm, ext_ref), (dst_hbm, dst_ref), (src_hbm, src_ref),
                (blk_hbm, blk_ref), (reg_hbm.at[0], reg_ref), (his_hbm.at[0], hist),
            )
        )
    ]

    def signal(s, y, x):
        pl.semaphore_signal(barrier, inc=1, device_id=(s, y, x), device_id_type=MESH)

    @pl.when(gy == 0)
    def _():
        for ref in (row_in, late_row_in):
            ref[:, 0] = jnp.zeros_like(ref[:, 0])

    @pl.when(gy == n_gy - 1)
    def _():
        for ref in (row_in, late_row_in):
            ref[:, 1] = jnp.zeros_like(ref[:, 1])

    signal(sect, gy, west)
    signal(sect, gy, east)

    @pl.when(is_ocean)
    def _():
        for t in range(1, n_gy):
            signal(0, lax.rem(gy + t, n_gy), gx)
        signal(1, gy, gx)

    @pl.when(is_atmos)
    def _():
        for t in range(n_gx):
            signal(0, gy, lax.rem(gx + t, n_gx))

        @pl.when(has_north)
        def _():
            signal(1, gy - 1, gx)

        @pl.when(has_south)
        def _():
            signal(1, gy + 1, gx)

    for load in loads:
        load.start()

    def halo_copies(i):
        return rim_copies(i, col_out, col_in, row_out, row_in, halo_send, halo_recv)

    def rim_copies(i, col_out, col_in, row_out, row_in, halo_send, halo_recv):
        def copy(j, source, target, y, x):
            return pltpu.make_async_remote_copy(
                src_ref=source, dst_ref=target, send_sem=halo_send.at[i, j], recv_sem=halo_recv.at[i, j],
                device_id=(sect, y, x), device_id_type=MESH,
            )

        return (
            copy(0, col_out.at[i, 0], col_in.at[i, 0], gy, east),
            copy(1, col_out.at[i, 1], col_in.at[i, 1], gy, west),
            copy(2, row_out.at[i, 1], row_in.at[i, 0], gy + 1, gx),
            copy(3, row_out.at[i, 0], row_in.at[i, 1], gy - 1, gx),
        )

    def prepare():
        for b in range(BANDS):
            rows = slice(b * SUB, (b + 1) * SUB)
            u = state[:, rows, :] * wet_f(rows)
            vee[:, rows, :] = u * dif[rows, :][None]
            u_hi[b], u_lo[b] = split(u.reshape(NC * SUB, NX))

    def wet_f(rows):
        return jnp.where(is_ocean, wet[rows, :].astype(F32), 1.0)[None]

    def rim_out(i):
        rim_pack(i, vee, NC, col_out, row_out)

    def rim_pack(i, vee, count, col_out, row_out):
        lane = iota((SUB, CELLS), 1)
        east_rim, west_rim = jnp.zeros((SUB, CELLS), F32), jnp.zeros((SUB, CELLS), F32)
        for c in range(count):
            row_out[i, 0, c : c + 1, :] = vee[c, :1, :]
            row_out[i, 1, c : c + 1, :] = vee[c, NY - 1 :, :]
            for b in range(BANDS):
                rows, at = slice(b * SUB, (b + 1) * SUB), b * NC + c
                east_rim = jnp.where(
                    lane == at, pltpu.roll(vee[c, rows, NX - CELLS :], (at + 1) % CELLS, 1), east_rim
                )
                west_rim = jnp.where(lane == at, pltpu.roll(vee[c, rows, :CELLS], at, 1) if at else vee[c, rows, :CELLS], west_rim)
        col_out[i, 0], col_out[i, 1] = east_rim, west_rim

    def rim_send(i, copies=halo_copies):
        e, w, s, n = copies(i)

        @pl.when(has_south)
        def _():
            s.start()

        @pl.when(has_north)
        def _():
            n.start()

        e.start()
        w.start()

    def rim_wait(i, copies=halo_copies):
        e, w, s, n = copies(i)
        e.wait()
        w.wait()

        @pl.when(has_south)
        def _():
            s.wait_send()
            n.wait_recv()

        @pl.when(has_north)
        def _():
            n.wait_send()
            s.wait_recv()

    def forced(coefs, fields):
        hi, lo = split(fields.reshape(FIELDS * SUB, NX))
        return mm(coefs, jnp.concatenate([hi, lo, hi], axis=0))

    def mix(k):
        for b in range(BANDS):
            rows = slice(b * SUB, (b + 1) * SUB)
            total = mm(k_hi[...], u_hi[b]) + mm(k_hi[...], u_lo[b]) + mm(k_lo[...], u_hi[b])
            total += forced(c_own[...], hist[k, :, rows, :])
            acc[:, rows, :] = total.reshape(NC, SUB, NX)

    def add_far(target, j, fields):
        for b in range(BANDS):
            rows = slice(b * SUB, (b + 1) * SUB)
            target[:, rows, :] += forced(c_far[j], fields[:, rows, :]).reshape(NC, SUB, NX)

    def laplace(i, c, vee, col_in, row_in):
        row, lane = iota((NY, NX), 0), iota((NY, NX), 1)
        v = vee[c]
        north, south = row_in[i, 0, c : c + 1, :], row_in[i, 1, c : c + 1, :]
        whole = (NY, NX)

        def column(j):
            bands = [col_in[i, j, :, b * NC + c : b * NC + c + 1] for b in range(BANDS)]
            return jnp.concatenate([jnp.broadcast_to(x, (SUB, CELLS)) for x in bands], axis=0)

        from_west, from_east = column(0), column(1)
        up = jnp.where(row == 0, jnp.broadcast_to(north, whole), pltpu.roll(v, 1, 0))
        down = jnp.where(row == NY - 1, jnp.broadcast_to(south, whole), pltpu.roll(v, NY - 1, 0))
        left = jnp.where(lane == 0, jnp.concatenate([from_west] * 2, axis=1), pltpu.roll(v, 1, 1))
        right = jnp.where(lane == NX - 1, jnp.concatenate([from_east] * 2, axis=1), pltpu.roll(v, NX - 1, 1))
        return ((up + down) + (left + right)) - 4.0 * v

    def spread(i):
        wet_all = jnp.where(is_ocean, wet[...].astype(F32), 1.0)
        for c in range(NC):
            state[c] = acc[c] + wet_all * state[c] + laplace(i, c, vee, col_in, row_in)

    def deliver(k):
        surface = []
        for b in range(BANDS):
            surface.append(
                mm(e_hi[...], u_hi[b]) + mm(e_hi[...], u_lo[b]) + mm(e_lo[...], u_hi[b])
            )
        parts = [
            surface[b][q * SUB : (q + 1) * SUB, h * CELLS : (h + 1) * CELLS]
            for q in range(FIELDS) for h in range(2) for b in range(BANDS)
        ]
        hi, lo = split(jnp.concatenate(parts, axis=0))
        regridded = mm(hi, r_hi[...]) + mm(lo, r_hi[...]) + mm(hi, r_lo[...])
        hi, lo = split(regridded)
        slots = mm(pick[...], hi) + mm(pick[...], lo)
        packed[k] = slots.reshape(tiles, CAP * FIELDS, CELLS)

        for y, x in farthest_first():
            pltpu.make_async_remote_copy(
                src_ref=packed.at[k, y * n_gx + x], dst_ref=arrived.at[k, me],
                send_sem=a2a_send.at[k], recv_sem=a2a_recv.at[k],
                device_id=(1, y, x), device_id_type=MESH,
            ).start()

    def receive(k):
        pltpu.make_async_copy(arrived.at[k], arrived.at[k], a2a_recv.at[k]).wait()
        hi, lo = split(arrived[k].reshape(tiles * CAP * FIELDS, CELLS))
        sums = mm(place[...], hi) + mm(place[...], lo)
        for q in range(FIELDS):
            for h in range(2):
                start = (q * 2 + h) * NY
                far[k, q, :, h * CELLS : (h + 1) * CELLS] = sums[start : start + NY]

    def late_copies(n):
        return rim_copies(n, late_col_out, late_col_in, late_row_out, late_row_in, late_send, late_recv)

    def late_start(n, fields):
        for j, field in enumerate(fields):
            for q in range(FIELDS):
                late_vee[j * FIELDS + q] = field[q] * dif[...]
        rim_pack(n, late_vee, len(fields) * FIELDS, late_col_out, late_row_out)
        rim_send(n, late_copies)

    def late_end(n, outputs):
        rim_wait(n, late_copies)
        for j, (ref, q_of) in enumerate(outputs):
            for q in range(FIELDS):
                ref[q] = q_of(laplace(n, j * FIELDS + q, late_vee, late_col_in, late_row_in), q)

    def atmosphere_end():
        first, second = late.at[0], late.at[1]
        receive(3)
        late_start(0, [far.at[3]])
        add_far(state, 3, far.at[3])
        late_end(0, [(first, lambda x, q: x)])
        receive(2)
        for q in range(FIELDS):
            x, r = first[q], far[2, q]
            first[q] = x + r
            second[q] = 3.0 * x + 2.0 * r
            far[3, q] = 3.0 * x + r
        late_start(1, [first, second])
        add_far(state, 2, far.at[3])
        late_end(1, [(first, lambda x, q: x), (second, lambda x, q: x)])
        receive(1)
        for q in range(FIELDS):
            r = far[1, q]
            first[q] += r
            second[q] += r
        late_start(2, [first])
        add_far(state, 1, second)
        late_end(2, [(first, lambda x, q: x)])
        receive(0)
        for q in range(FIELDS):
            first[q] += far[0, q]
        add_far(state, 0, first)

    def far_copy(k, target_sect):
        return pltpu.make_async_remote_copy(
            src_ref=his_hbm.at[0, k], dst_ref=far.at[k], send_sem=far_send.at[k], recv_sem=far_recv.at[k],
            device_id=(target_sect, gy, gx), device_id_type=MESH,
        )

    for load in loads[:3]:
        load.wait()
    prepare()
    rim_out(0)

    beside = jnp.where(has_north, 1, 0) + jnp.where(has_south, 1, 0)
    pl.semaphore_wait(barrier, 2 + jnp.where(is_ocean, n_gx + n_gy - 1, 1 + beside))
    rim_send(0)

    @pl.when(is_ocean)
    def _():
        for t in range(1, n_gy):
            pl.semaphore_signal(
                ready, inc=1, device_id=(0, lax.rem(gy + t, n_gy), gx), device_id_type=MESH
            )

    @pl.when(is_atmos)
    def _():
        for k in range(STEPS - 1, -1, -1):
            far_copy(k, 0).start()

    for load in loads[3:]:
        load.wait()

    k_hi[...], k_lo[...] = widen(mix_ref[...].T)

    def triple(small):
        hi, lo = widen(small)
        return jnp.concatenate([hi, hi, lo], axis=1)

    c_own[...] = triple(cou_ref[:FIELDS, :].T)
    c_far[0] = triple(cou_ref[FIELDS:, :].T)

    @pl.when(is_ocean)
    def _():
        e_hi[...], e_lo[...] = widen(ext_ref[...])
        r_hi[...], r_lo[...] = split(reg_ref[...])
        entries = dst_ref.shape[1]
        dest = dst_ref[pl.ds(me, 1), :]
        source = block_place(src_ref[pl.ds(me, 1), :])
        dest_row = jnp.broadcast_to(dest, (entries, entries))
        dest_col = dest_row.T
        square = (entries, entries)
        earlier = (dest_row == dest_col) & (iota(square, 0) < iota(square, 1))
        rank = jnp.sum(jnp.where(earlier, 1, 0), axis=0, keepdims=True)
        position = dest * CAP + rank
        slots = tiles * CAP * FIELDS
        goes = onehot(jnp.broadcast_to(position, (slots, entries)) == iota((slots, entries), 0) // FIELDS)
        wide = FIELDS * BLOCKS
        reads = onehot(jnp.broadcast_to(source, (wide, entries)) == iota((wide, entries), 0) % BLOCKS)
        field = iota((slots, wide), 0) % FIELDS == iota((slots, wide), 1) // BLOCKS
        pick[...] = jnp.where(field, mm_nt(goes, reads), 0.0).astype(BF16)

    @pl.when(is_atmos)
    def _():
        entries = dst_ref.shape[1]
        square = (entries, entries)
        match = dst_ref[...] == me
        before = onehot(iota(square, 0) < iota(square, 1))
        rank = mm(onehot(match), before)
        block = (block_place(blk_ref[...]) + 1).astype(F32)
        slots = tiles * CAP * FIELDS
        spread = onehot(iota((tiles, slots), 1) // (CAP * FIELDS) == iota((tiles, slots), 0))
        which = (iota((SUB, slots), 1) // FIELDS) % CAP
        code = jnp.zeros((SUB, slots), F32)
        for r in range(CAP):
            value = jnp.where(match & (rank == r), block, 0.0).astype(BF16)
            row = mm_nt(jnp.ones((SUB, entries), BF16), value)
            code = jnp.where(which == r, mm(row.astype(BF16), spread), code)
        wide = FIELDS * BLOCKS
        shape = (wide, slots)
        lands = jnp.broadcast_to(code[:1], shape) == (iota(shape, 0) % BLOCKS + 1).astype(F32)
        field = iota(shape, 0) // BLOCKS == iota(shape, 1) % FIELDS
        place[...] = onehot(lands & field)
        mixed = cou_ref[FIELDS:, :].T
        for j in range(1, STEPS):
            mixed += jnp.dot(
                mix_ref[...].T, mixed, precision=lax.Precision.HIGHEST, preferred_element_type=F32
            )
            c_far[j] = triple(mixed)

    def step(i, carry):
        k = STEPS - 1 - i
        mix(k)

        @pl.when(is_ocean)
        def _():
            far_copy(k, 1).wait_recv()
            add_far(acc, 0, far.at[k])

        rim_wait(i)
        spread(i)

        @pl.when(i < STEPS - 1)
        def _():
            prepare()
            rim_out(i + 1)
            rim_send(i + 1)

        @pl.when(is_ocean)
        def _():
            @pl.when(i == STEPS - 1)
            def _():
                prepare()

            @pl.when(i == 0)
            def _():
                pl.semaphore_wait(ready, n_gy - 1)

            deliver(k)

        return carry

    lax.fori_loop(0, STEPS, step, 0)

    @pl.when(is_atmos)
    def _():
        atmosphere_end()

    @pl.when(is_ocean)
    def _():
        for k in range(STEPS):
            pltpu.make_async_copy(packed.at[k], packed.at[k], a2a_send.at[k]).wait()

    @pl.when(is_atmos)
    def _():
        for k in range(STEPS):
            far_copy(k, 0).wait_send()


def body(n_gy, n_gx, adj, dif, mix, cou, his, ext, msk, reg, dst, src, blk):
    tiles = n_gy * n_gx
    entries = src.shape[0] // tiles
    tables = [x.reshape(tiles, entries) for x in (dst, src, blk)]
    anywhere = pl.BlockSpec(memory_space=pl.ANY)
    rows, slots, wide = NC * SUB, tiles * CAP * FIELDS, FIELDS * BLOCKS
    dma = pltpu.SemaphoreType.DMA
    return pl.pallas_call(
        functools.partial(kernel, n_gy, n_gx),
        out_shape=pltpu.VMEM(adj.shape, F32),
        in_specs=[anywhere] * 11,
        out_specs=pl.BlockSpec(memory_space=pltpu.VMEM),
        scratch_shapes=[
            pltpu.VMEM((NC, NC), F32),
            pltpu.VMEM((2 * FIELDS, NC), F32),
            pltpu.VMEM((FIELDS, NC), F32),
            pltpu.VMEM((CELLS, CELLS), F32),
            pltpu.VMEM((tiles, entries), jnp.int32),
            pltpu.VMEM((tiles, entries), jnp.int32),
            pltpu.VMEM((tiles, entries), jnp.int32),
            pltpu.VMEM((NY, NX), jnp.int32),
            pltpu.VMEM((NY, NX), F32),
            pltpu.VMEM((STEPS, FIELDS, NY, NX), F32),
            pltpu.VMEM((STEPS, FIELDS, NY, NX), F32),
            pltpu.VMEM((NC, NY, NX), F32),
            pltpu.VMEM((NC, NY, NX), F32),
            pltpu.VMEM((BANDS, rows, NX), BF16),
            pltpu.VMEM((BANDS, rows, NX), BF16),
            pltpu.VMEM((rows, rows), BF16),
            pltpu.VMEM((rows, rows), BF16),
            pltpu.VMEM((rows, 3 * FIELDS * SUB), BF16),
            pltpu.VMEM((STEPS, rows, 3 * FIELDS * SUB), BF16),
            pltpu.VMEM((FIELDS * SUB, rows), BF16),
            pltpu.VMEM((FIELDS * SUB, rows), BF16),
            pltpu.VMEM((CELLS, CELLS), BF16),
            pltpu.VMEM((CELLS, CELLS), BF16),
            pltpu.VMEM((slots, wide), BF16),
            pltpu.VMEM((wide, slots), BF16),
            pltpu.VMEM((STEPS, tiles, CAP * FIELDS, CELLS), F32),
            pltpu.VMEM((STEPS, tiles, CAP * FIELDS, CELLS), F32),
            pltpu.VMEM((STEPS, 2, NC, NX), F32),
            pltpu.VMEM((STEPS, 2, NC, NX), F32),
            pltpu.VMEM((STEPS, 2, SUB, CELLS), F32),
            pltpu.VMEM((STEPS, 2, SUB, CELLS), F32),
            pltpu.VMEM((2, FIELDS, NY, NX), F32),
            pltpu.VMEM((2 * FIELDS, NY, NX), F32),
            pltpu.VMEM((STEPS - 1, 2, 2 * FIELDS, NX), F32),
            pltpu.VMEM((STEPS - 1, 2, 2 * FIELDS, NX), F32),
            pltpu.VMEM((STEPS - 1, 2, SUB, CELLS), F32),
            pltpu.VMEM((STEPS - 1, 2, SUB, CELLS), F32),
            dma((11,)), pltpu.SemaphoreType.REGULAR, dma((STEPS,)), dma((STEPS,)), dma((STEPS, 4)), dma((STEPS, 4)),
            dma((STEPS,)), dma((STEPS,)), dma((STEPS - 1, 4)), dma((STEPS - 1, 4)),
        ],
        compiler_params=pltpu.CompilerParams(
            collective_id=0, has_side_effects=True, vmem_limit_bytes=60 * 1024 * 1024
        ),
    )(adj, dif, mix, cou.swapaxes(1, 2), his, ext, msk, reg, *tables)


def solution(mesh):
    placed = (
        P("sect", None, "gy", "gx"), P("sect", "gy", "gx"), P("sect", None, None), P("sect", None, None),
        P("sect", None, None, "gy", "gx"), P(), P("gy", "gx"), P(("gy", "gx"), None, None), P(), P(), P(),
    )
    return jax.shard_map(
        functools.partial(body, mesh.shape["gy"], mesh.shape["gx"]),
        mesh=mesh, in_specs=placed, out_specs=P("sect", None, "gy", "gx"), check_vma=False,
    )
```
